32 devices in a mesh: groups: 2 (over y), fsdp: 8 (over z, x), blk: 2 (over core).
Axes of the slice: x: 2, y: 2, z: 4, core: 2. Of those that a mesh axis runs over, the one named last changes fastest.
Arguments:
- block_input: bfloat16 [8192, 5120], P(('groups', 'fsdp', 'blk')), parts along dimension 0, may hold values from -3 to 3
- gate: float32 [10240], P('groups'), parts along dimension 0, may hold values from -6 to 6
- q_fresh: bfloat16 [8192, 2560], P(('groups', 'fsdp', 'blk')), parts along dimension 0, may hold values from -48.5 to 48.5
- kv_fresh: bfloat16 [8192, 2, 2560], P(('groups', 'fsdp', 'blk')), parts along dimension 0, may hold values from -6 to 6
- kv_cache: bfloat16 [8192, 2, 2560], P(('groups', 'fsdp', 'blk')), parts along dimension 0, may hold values from -6 to 6
- active_list: int32 [16, 2, 2], P(('groups', 'fsdp')), parts along dimension 0, may hold values from 0 to 1, as said below
- active_count: int32 [16, 2], P(('groups', 'fsdp')), parts along dimension 0, may hold values from 0 to 2, as said below
- key_list: int32 [16, 4, 3], P(('groups', 'fsdp')), parts along dimension 0, may hold values from 0 to 3, as said below
- out_weight: bfloat16 [2560, 5120], P('fsdp'), may hold values from -0.125 to 0.125
Outputs:
- block_output: bfloat16 [8192, 5120], P(('groups', 'fsdp', 'blk')), parts along dimension 0
The draws below stay inside these ranges and needn't reach their ends.
There are 2 independent parts, one for each index of `groups`. The reference program is written for one: setup_inputs(seed, part) draws one part's arguments, and reference() takes and returns one part's arrays. A program takes and returns all parts, laid end to end along the dimension named above; an argument that names none is the same for every part. Nothing has to cross between parts.
Inputs may be any that keep to these rules, and one draw needn't show every extreme that they name: `active_list`: each row [f, b] holds every tile number once; its first active_count[f, b] entries are the active tiles. `active_count`: some token block has all 2 tiles active. `key_list`: entry [f, g] holds 3 different tile ids of group f, the first one being g.
All inputs are finite; a program needn't handle non-finite values.
Results may differ from the reference program's by a relative error of at most 0.0034.
Values may be sent and summed in bfloat16 or wider, within the bound.
A program may use at most 128 MiB of HBM per device.

```python
import math
import jax
import jax.numpy as jnp
from jax import lax

D = 5120
HEADS = 20
HEAD_DIM = 128
TILE = 128
TILES_DEV = 2
HD = 2560
TOK_DEV = 256
GROUP_TILES = 4
KEY_TILES = 3
TOKENS = 4096
N_FSDP = 8
N_BLK = 2


def fresh_pair(key):
    base_key = jax.random.fold_in(key, 37)
    query_key, keys_key, values_key = jax.random.split(base_key, 3)
    queries = jnp.clip(2.0 * jax.random.normal(query_key, (TOKENS, HD), jnp.float32), -8.0, 8.0)
    key_rows = jnp.clip(jax.random.normal(keys_key, (TOKENS, HD), jnp.float32), -6.0, 6.0)
    value_rows = jnp.clip(jax.random.normal(values_key, (TOKENS, HD), jnp.float32), -6.0, 6.0)
    return (queries, jnp.stack([key_rows, value_rows], axis=1))


def draw_q_fresh(key, part):
    return fresh_pair(key)[0].astype(jnp.bfloat16)


def draw_kv_fresh(key, part):
    return fresh_pair(key)[1].astype(jnp.bfloat16)


def active_pair(key):
    base_key = jax.random.fold_in(key, 11)
    count_key, pick_key, order_key = jax.random.split(base_key, 3)
    block_count = N_FSDP * N_BLK
    counts = jax.random.randint(count_key, (block_count,), 0, TILES_DEV + 1)
    full_block = jax.random.randint(pick_key, (), 0, block_count)
    counts = jnp.where(jnp.arange(block_count, dtype=jnp.int32) == full_block, TILES_DEV, counts)
    ranking = jax.random.randint(order_key, (block_count, TILES_DEV), 0, 1 << 20) * TILES_DEV + jnp.arange(TILES_DEV, dtype=jnp.int32)[None, :]
    ordering = jnp.argsort(ranking, axis=1, stable=True).astype(jnp.int32)
    return (ordering.reshape(N_FSDP, N_BLK, TILES_DEV), counts.astype(jnp.int32).reshape(N_FSDP, N_BLK))


def draw_active_list(key, part):
    return active_pair(key)[0]


def draw_active_count(key, part):
    return active_pair(key)[1]


def draw_key_list(key, part):
    base_key = jax.random.fold_in(key, 23)
    tile_ids = jnp.arange(GROUP_TILES, dtype=jnp.int32)
    ranking = jax.random.randint(base_key, (N_FSDP, GROUP_TILES, GROUP_TILES), 0, 1 << 20) * GROUP_TILES + tile_ids[None, None, :]
    ranking = jnp.where(tile_ids[None, :, None] == tile_ids[None, None, :], -1, ranking)
    ordering = jnp.argsort(ranking, axis=2, stable=True).astype(jnp.int32)
    return ordering[:, :, :KEY_TILES]


def levels(rng, dims, cuts, low, top_value):
    level, own = 1.0, jax.random.fold_in(rng, 6)
    for dim, shards_of in cuts:
        draws = jnp.exp(jax.random.uniform(jax.random.fold_in(own, dim), (shards_of,), jnp.float32, low / len(cuts), top_value / len(cuts)))
        level = level * jnp.repeat(draws, dims[dim] // shards_of).reshape([-1 if axis == dim else 1 for axis in range(len(dims))])
    return level


def scatter_about(rng, shape, deviation, bound, shards=(), held_as=jnp.bfloat16):
    result = jax.random.normal(rng, shape, jnp.float32) * deviation
    if len(shards) > 0:
        result = levels(rng, shape, shards, -0.22, 0.18) * result
    return jnp.clip(result, min=-bound, max=bound).astype(held_as)


def setup_inputs(seed: int = 0, part: int = 0) -> dict:
    seeds = jax.random.split(jax.random.key(seed), 10)
    own_keys = jax.random.split(jax.random.fold_in(seeds[9], part), 10)
    return {
        "block_input": scatter_about(own_keys[0], (TOKENS, D), 0.5, 3.0, ((0, 16),)),
        "gate": scatter_about(own_keys[1], (D,), 1.5, 6.0, (), jnp.float32),
        "q_fresh": draw_q_fresh(jax.random.fold_in(jax.random.fold_in(seeds[9], part), 71), part),
        "kv_fresh": draw_kv_fresh(jax.random.fold_in(jax.random.fold_in(seeds[9], part), 71), part),
        "kv_cache": scatter_about(own_keys[4], (TOKENS, 2, HD), 1.0, 6.0, ((0, 16),)),
        "active_list": draw_active_list(jax.random.fold_in(jax.random.fold_in(seeds[9], part), 71), part),
        "active_count": draw_active_count(jax.random.fold_in(jax.random.fold_in(seeds[9], part), 71), part),
        "key_list": draw_key_list(jax.random.fold_in(jax.random.fold_in(seeds[9], part), 71), part),
        "out_weight": scatter_about(seeds[8], (HD, D), HD ** -0.5, 0.125, ((0, 8),)),
    }


MASKED = -1e+30

def block_partial(query_tile, key_rows, value_rows, allowed):
    tile_rows = query_tile.shape[0]
    query3 = query_tile.astype(jnp.float32).reshape(tile_rows, HEADS, HEAD_DIM)
    key3 = key_rows.astype(jnp.float32).reshape(key_rows.shape[0], HEADS, HEAD_DIM)
    value3 = value_rows.astype(jnp.float32).reshape(value_rows.shape[0], HEADS, HEAD_DIM)
    scores = jnp.einsum('qhd,khd->hqk', query3, key3) / math.sqrt(HEAD_DIM)
    scores = jnp.where(allowed[None, None, :], scores, MASKED)
    row_max = lax.optimization_barrier(jnp.max(scores, axis=2))
    exp_terms = jnp.where(allowed[None, None, :], jnp.exp(scores - row_max[:, :, None]), 0.0)
    row_total = lax.optimization_barrier(jnp.sum(exp_terms, axis=2))
    weights = lax.optimization_barrier(exp_terms.astype(jnp.bfloat16)).astype(jnp.float32)
    block_out = jnp.einsum('hqk,khd->hqd', weights, value3)
    return (block_out, row_max, row_total)

def reference(block_input, gate, q_fresh, kv_fresh, kv_cache, active_list, active_count, key_list, out_weight):
    block_count = N_FSDP * N_BLK
    slot_ids = jnp.arange(TILES_DEV, dtype=jnp.int32)
    tile_lists = active_list.reshape(block_count, TILES_DEV)
    tile_counts = active_count.reshape(block_count)
    listed = (tile_lists[:, :, None] == slot_ids[None, None, :]) & (slot_ids[None, :, None] < tile_counts[:, None, None])
    tile_active = jnp.any(listed, axis=1).reshape(block_count * TILES_DEV)
    row_active = jnp.repeat(tile_active, TILE)
    resident = jnp.where(row_active[:, None, None], kv_fresh, kv_cache)

    def one_tile(tile_index):
        group_id = tile_index // GROUP_TILES
        group_tile = tile_index % GROUP_TILES
        row_start = tile_index * TILE
        input_tile = lax.dynamic_slice_in_dim(block_input, row_start, TILE, 0)

        def compute_tile():
            query_tile = lax.dynamic_slice_in_dim(q_fresh, row_start, TILE, 0)
            listed_keys = key_list[group_id, group_tile]
            partials = []
            for key_side in range(N_BLK):
                row_base = (group_id * N_BLK + key_side) * TOK_DEV
                block_kv = lax.dynamic_slice_in_dim(resident, row_base, TOK_DEV, 0)
                key_tiles = key_side * TILES_DEV + slot_ids
                allowed_tiles = jnp.any(key_tiles[:, None] == listed_keys[None, :], axis=1)
                allowed = jnp.repeat(allowed_tiles, TILE)
                partials.append(block_partial(query_tile, block_kv[:, 0], block_kv[:, 1], allowed))
            joint_max = jnp.maximum(partials[0][1], partials[1][1])
            scale_zero = jnp.exp(partials[0][1] - joint_max)
            scale_one = jnp.exp(partials[1][1] - joint_max)
            summed = partials[0][0] * scale_zero[:, :, None] + partials[1][0] * scale_one[:, :, None]
            denom = partials[0][2] * scale_zero + partials[1][2] * scale_one
            attended = (summed / denom[:, :, None]).transpose(1, 0, 2).reshape(TILE, HD).astype(jnp.bfloat16)
            projected = jnp.dot(attended, out_weight, preferred_element_type=jnp.float32)
            return (input_tile.astype(jnp.float32) + gate[None, :] * projected).astype(jnp.bfloat16)

        def skip_tile():
            return input_tile
        return lax.cond(tile_active[tile_index], compute_tile, skip_tile)
    tiles = lax.map(one_tile, jnp.arange(TOKENS // TILE, dtype=jnp.int32))
    return tiles.reshape(TOKENS, D)
```

```python
import functools
import math

import jax
import jax.numpy as jnp
from jax import lax
from jax.experimental import pallas as pl
from jax.experimental.pallas import tpu as pltpu
from jax.sharding import PartitionSpec as P

HEADS = 20
HEAD_DIM = 128


MASKED = -1e30


def swapped(block, axis, apart):
    count = lax.axis_size(axis)
    route = []
    for low in range(count):
        high = low | 1 << apart
        if high != low and high < count:
            route += [(low, high), (high, low)]
    return lax.ppermute(block, axis, route)


def tile_flags(tile_list, tile_count):
    slot_ids = jnp.arange(tile_list.shape[0], dtype=jnp.int32)
    listed = (tile_list[:, None] == slot_ids[None, :]) & (slot_ids[:, None] < tile_count)
    return jnp.any(listed, axis=0)


def block_partial(query_tile, key_rows, value_rows, allowed):
    tile_rows = query_tile.shape[0]
    query3 = query_tile.reshape(tile_rows, HEADS, HEAD_DIM)
    key3 = key_rows.reshape(key_rows.shape[0], HEADS, HEAD_DIM)
    value3 = value_rows.reshape(value_rows.shape[0], HEADS, HEAD_DIM)
    scores = jnp.einsum(
        "qhd,khd->hqk", query3, key3, preferred_element_type=jnp.float32
    ) / math.sqrt(HEAD_DIM)
    scores = jnp.where(allowed[None, None, :], scores, MASKED)
    row_max = jnp.max(scores, axis=2)
    exp_terms = jnp.where(allowed[None, None, :], jnp.exp(scores - row_max[:, :, None]), 0.0)
    row_total = jnp.sum(exp_terms, axis=2)
    weights = exp_terms.astype(jnp.bfloat16)
    block_out = jnp.einsum("hqk,khd->hqd", weights, value3, preferred_element_type=jnp.float32)
    return (block_out, row_max, row_total)


def attend_block(
    queries, tile_list, tile_count, query_side, key_rows, value_rows, key_side, key_table
):
    tiles_dev = tile_list.shape[0]
    tile_rows = queries.shape[0] // tiles_dev
    slot_ids = jnp.arange(tiles_dev, dtype=jnp.int32)
    key_tiles = key_side * tiles_dev + slot_ids
    init_state = (
        jnp.zeros((tiles_dev, HEADS, tile_rows, HEAD_DIM), jnp.float32),
        jnp.full((tiles_dev, HEADS, tile_rows), MASKED, jnp.float32),
        jnp.zeros((tiles_dev, HEADS, tile_rows), jnp.float32),
    )

    def one_slot(slot_idx, carry_state):
        tile_pos = tile_list[slot_idx]
        query_tile = lax.dynamic_slice_in_dim(queries, tile_pos * tile_rows, tile_rows, 0)
        listed = key_table[query_side * tiles_dev + tile_pos]
        allowed_tiles = jnp.any(key_tiles[:, None] == listed[None, :], axis=1)
        allowed = jnp.repeat(allowed_tiles, tile_rows, total_repeat_length=tiles_dev * tile_rows)
        partial_value = block_partial(query_tile, key_rows, value_rows, allowed)
        return tuple(
            (whole.at[tile_pos].set(piece) for whole, piece in zip(carry_state, partial_value))
        )

    return lax.fori_loop(0, tile_count, one_slot, init_state)


def merge_states(earlier, later_state):
    out_one, max_one, total_one = earlier
    out_two, max_two, total_two = later_state
    joint_max = jnp.maximum(max_one, max_two)
    scale_one = jnp.exp(max_one - joint_max)
    scale_two = jnp.exp(max_two - joint_max)
    summed = out_one * scale_one[..., None] + out_two * scale_two[..., None]
    return (summed, total_one * scale_one + total_two * scale_two)


def local(
    block_input, gate, q_fresh, kv_fresh, kv_cache, active_list, active_count, key_list, out_weight
):
    own_side = lax.axis_index("blk")
    other_side = 1 - own_side
    tiles_dev = active_list.shape[2]
    tok_dev = block_input.shape[0]
    tile_rows = tok_dev // tiles_dev
    own_list = active_list[0, own_side]
    own_count = active_count[0, own_side]
    flags = tile_flags(own_list, own_count)
    row_flags = jnp.repeat(flags, tile_rows, total_repeat_length=tok_dev)
    resident = jnp.where(row_flags[:, None, None], kv_fresh, kv_cache)
    key_table = key_list[0]
    own_state = attend_block(
        q_fresh, own_list, own_count, own_side, resident[:, 0], resident[:, 1], own_side, key_table
    )
    other_kv = swapped(resident, "blk", 0)
    other_state = attend_block(
        q_fresh,
        own_list,
        own_count,
        own_side,
        other_kv[:, 0],
        other_kv[:, 1],
        other_side,
        key_table,
    )
    summed, denom = merge_states(own_state, other_state)
    denom = jnp.where(flags[:, None, None], denom, 1.0)
    attended = (
        (summed / denom[..., None])
        .transpose(0, 2, 1, 3)
        .reshape(tok_dev, HEADS * HEAD_DIM)
        .astype(jnp.bfloat16)
    )
    half_cols = out_weight.shape[1] // 2
    own_cols = lax.dynamic_slice_in_dim(out_weight, own_side * half_cols, half_cols, 1)
    half_weight = lax.all_gather(own_cols, "fsdp", axis=0, tiled=True)
    partner_rows = swapped(attended, "blk", 0)
    own_part = jnp.dot(attended, half_weight, preferred_element_type=jnp.float32)
    partner_part = jnp.dot(partner_rows, half_weight, preferred_element_type=jnp.float32)
    returned = swapped(partner_part, "blk", 0)
    projected = jnp.where(
        own_side == 0,
        jnp.concatenate([own_part, returned], axis=1),
        jnp.concatenate([returned, own_part], axis=1),
    )
    mixed = block_input.astype(jnp.float32) + gate[None, :] * projected
    return jnp.where(row_flags[:, None], mixed.astype(jnp.bfloat16), block_input)

MESH = pl.DeviceIdType.MESH
CHUNKS = 10
LINE = 2


def fused(
    depth,
    active_list,
    active_count,
    key_list,
    block_hbm,
    gate_ref,
    q_hbm,
    k_hbm,
    v_hbm,
    w_hbm,
    out_hbm,
    weight,
    queries,
    keys,
    values,
    attended,
    mixed_in,
    mixed_out,
    mask,
    load_sem,
    w_sem,
    pair_send,
    pair_recv,
    send_sem,
    recv_sem,
    store_sem,
    out_send,
    out_recv,
):
    me = lax.axis_index("fsdp")
    z, x = me // LINE, me % LINE
    y = lax.axis_index("groups")
    b = lax.axis_index("blk")
    rows = w_hbm.shape[0]
    tok = q_hbm.shape[0]
    half = w_hbm.shape[1] // 2
    width = half // CHUNKS
    tiles = active_list.shape[2]
    tile_rows = tok // tiles
    heads = q_hbm.shape[1] // HEAD_DIM
    mine = pl.multiple_of(b * half, 128)
    theirs = pl.multiple_of((1 - b) * half, 128)

    barrier = pltpu.get_barrier_semaphore()
    targets = (
        (z < depth - 1, {"fsdp": me + LINE}),
        (z > 0, {"fsdp": me - LINE}),
        (None, {"fsdp": z * LINE + 1 - x}),
        (None, {"groups": 1 - y}),
    )
    core = {"blk": 1 - b}

    def when(cond, body):
        if cond is None:
            body()
        else:
            pl.when(cond)(body)

    def greet(device):
        pl.semaphore_signal(barrier, inc=1, device_id=device, device_id_type=MESH)

    for cond, device in targets + ((None, core),):
        when(cond, functools.partial(greet, device))

    def own_weight(c):
        return pltpu.make_async_copy(
            w_hbm.at[:, pl.ds(pl.multiple_of(mine + c * width, 128), width)],
            weight.at[c, pl.ds(pl.multiple_of(me * rows, 16), rows), :],
            w_sem.at[c],
        )

    def stream(i):
        return jnp.where(i == 0, y, jnp.where(i < 3, 1 + 2 * y + i, 3 + i))

    def passive(i):
        return jnp.where(i == 0, 1 - y, 3 - 2 * y + i)

    def every(i):
        return jnp.where(i < 7, stream(i), passive(i - 7))

    for i in range(CHUNKS):
        own_weight(every(jnp.int32(i))).start()

    loads = [
        pltpu.make_async_copy(q_hbm, queries, load_sem.at[0]),
        pltpu.make_async_copy(k_hbm, keys.at[pl.ds(0, tok)], load_sem.at[1]),
        pltpu.make_async_copy(v_hbm, values.at[pl.ds(0, tok)], load_sem.at[2]),
        pltpu.make_async_copy(
            block_hbm.at[:, pl.ds(mine, half)], mixed_in.at[pl.ds(0, tok)], load_sem.at[3]
        ),
    ]
    for load in loads:
        load.start()

    pl.semaphore_wait(barrier, 3 + (z > 0).astype(jnp.int32) + (z < depth - 1).astype(jnp.int32))

    def to_core(src, dst, index):
        return pltpu.make_async_remote_copy(
            src_ref=src,
            dst_ref=dst,
            send_sem=pair_send.at[index],
            recv_sem=pair_recv.at[index],
            device_id=core,
            device_id_type=MESH,
        )

    swaps = [
        to_core(k_hbm, keys.at[pl.ds(tok, tok)], 0),
        to_core(v_hbm, values.at[pl.ds(tok, tok)], 1),
        to_core(block_hbm.at[:, pl.ds(theirs, half)], mixed_in.at[pl.ds(tok, tok)], 2),
    ]
    give = to_core(attended.at[pl.ds(0, tok)], attended.at[pl.ds(tok, tok)], 3)
    for swap in swaps:
        swap.start()

    def shard_copy(c, s, way):
        block = weight.at[c, pl.ds(pl.multiple_of(s * rows, 16), rows), :]
        return pltpu.make_async_remote_copy(
            src_ref=block,
            dst_ref=block,
            send_sem=send_sem.at[c, s, way],
            recv_sem=recv_sem.at[c, s],
            device_id=targets[way][1],
            device_id_type=MESH,
        )

    def visit(c, first, over_y, dz, dx, done):
        s = (z + dz) * LINE + (x if dx == 0 else 1 - x)
        ways = []
        if first == "z":
            if dx == 0:
                ways += [0] if dz <= 0 else []
                ways += [1] if dz >= 0 else []
                ways += [2]
        else:
            ways += [2] if (dz, dx) == (0, 0) else []
            ways += [0] if dz <= 0 else []
            ways += [1] if dz >= 0 else []

        def body():
            if (dz, dx) == (0, 0):
                if not done:
                    own_weight(c).wait()
            elif not done:
                shard_copy(c, s, 2).wait_recv()

            def act(way):
                copy = shard_copy(c, s, way)
                if done:
                    copy.wait_send()
                else:
                    copy.start()

            for way in ways:
                when(targets[way][0], functools.partial(act, way))
            if (dz, dx) != (0, 0) and over_y is not False:
                when(None if over_y is True else over_y, functools.partial(act, 3))

        if dz < 0:
            pl.when(z + dz >= 0)(body)
        elif dz > 0:
            pl.when(z + dz < depth)(body)
        else:
            body()

    def offsets(level):
        found = []
        for dx in range(LINE):
            far = level - dx
            if 0 <= far < depth:
                found += [(0, dx)] if far == 0 else [(-far, dx), (far, dx)]
        return found

    levels = depth + LINE - 1

    def step_x(level, done=False):
        for dz, dx in offsets(level):
            visit(y, "x", True, dz, dx, done)

    def step_z(i, level, done=False):
        for dz, dx in offsets(level):
            visit(stream(i), "z", i < 3, dz, dx, done)

    step_x(0)
    pl.loop(1, 7)(lambda i: step_z(i, 0))

    for load in loads[:3]:
        load.wait()
    for swap in swaps[:2]:
        swap.wait_recv()

    for a in range(tiles):
        for t in range(2 * tiles):
            side = b if t < tiles else 1 - b
            tile_id = side * tiles + t % tiles
            listed = jnp.int32(0)
            for slot in range(key_list.shape[2]):
                hit = key_list[0, b * tiles + a, slot] == tile_id
                listed = jnp.where(hit, jnp.int32(1), listed)
            mask[pl.ds(a * tile_rows, tile_rows), pl.ds(t * tile_rows, tile_rows)] = jnp.full(
                (tile_rows, tile_rows), listed.astype(jnp.float32), jnp.float32
            )

    def attend(h):
        cols = pl.ds(pl.multiple_of(h * HEAD_DIM, 128), HEAD_DIM)
        query = queries[:, cols]
        parts = []
        for side in range(2):
            span = pl.ds(side * tok, tok)
            scores = lax.dot_general(
                query,
                keys[span, cols],
                (((1,), (1,)), ((), ())),
                preferred_element_type=jnp.float32,
            ) * (1.0 / math.sqrt(HEAD_DIM))
            allowed = mask[:, span] > 0.5
            scores = jnp.where(allowed, scores, MASKED)
            top = jnp.max(scores, axis=1, keepdims=True)
            terms = jnp.where(allowed, jnp.exp(scores - top), 0.0)
            total = jnp.sum(terms, axis=1, keepdims=True)
            part = jnp.dot(
                terms.astype(jnp.bfloat16), values[span, cols], preferred_element_type=jnp.float32
            )
            parts.append((part, top, total))
        (out0, max0, sum0), (out1, max1, sum1) = parts
        joint = jnp.maximum(max0, max1)
        scale0 = jnp.exp(max0 - joint)
        scale1 = jnp.exp(max1 - joint)
        denom = sum0 * scale0 + sum1 * scale1
        result = (out0 * scale0 + out1 * scale1) / denom
        attended[pl.ds(0, tok), cols] = result.astype(jnp.bfloat16)

    def attend_range(low, high):
        pl.loop(low, high)(attend)

    each = heads // 7
    first = heads - 6 * each
    step_x(1)
    attend_range(0, first)

    @pl.loop(1, 7)
    def _(i):
        step_z(i, 1)
        attend_range(first + (i - 1) * each, first + i * each)

    give.start()
    for level in range(2, levels - 1):
        step_x(level)
        pl.loop(1, 7)(functools.partial(step_z, level=level))

    loads[3].wait()
    swaps[2].wait_recv()
    give.wait_recv()

    def is_active(side, a):
        found = jnp.int32(0)
        for slot in range(tiles):
            hit = (active_list[0, side, slot] == a) & (slot < active_count[0, side])
            found = jnp.where(hit, jnp.int32(1), found)
        return found

    flags = [is_active(side, a) for side in (b, 1 - b) for a in range(tiles)]

    def out_copies(c):
        cols = pl.ds(pl.multiple_of(mine + c * width, 128), width)
        return (
            pltpu.make_async_copy(
                mixed_out.at[c, pl.ds(0, tok), :], out_hbm.at[:, cols], store_sem.at[c]
            ),
            pltpu.make_async_remote_copy(
                src_ref=mixed_out.at[c, pl.ds(tok, tok), :],
                dst_ref=out_hbm.at[:, cols],
                send_sem=out_send.at[c],
                recv_sem=out_recv.at[c],
                device_id=core,
                device_id_type=MESH,
            ),
        )

    def project(j):
        i = jnp.where(j < 3, j, jnp.where(j < 6, j + 4, j - 3))
        c = every(i)

        @pl.when(j == 0)
        def _():
            step_x(levels - 1)

        @pl.when((j == 1) | (j == 2) | (j >= 6))
        def _():
            step_z(i, levels - 1)

        @pl.when((j >= 3) & (j < 6))
        def _():
            own_weight(c).wait()
            for s in range(depth * LINE):
                pl.when(me != s)(lambda s=s: shard_copy(c, s, 3).wait_recv())

        projected = jnp.dot(attended[...], weight[c], preferred_element_type=jnp.float32)
        gate = gate_ref[:, pl.ds(pl.multiple_of(mine + c * width, 128), width)]
        cols = pl.ds(pl.multiple_of(c * width, 128), width)
        for place, flag in enumerate(flags):
            span = pl.ds(place * tile_rows, tile_rows)
            before = mixed_in[span, cols].astype(jnp.float32)
            part = projected[place * tile_rows : (place + 1) * tile_rows]
            mixed = jnp.where(flag > 0, before + gate * part, before)
            mixed_out[c, span, :] = mixed.astype(jnp.bfloat16)
        for copy in out_copies(c):
            copy.start()

    pl.loop(0, CHUNKS)(project)

    for swap in swaps + [give]:
        swap.wait_send()
    for level in range(levels):
        step_x(level, done=True)
        pl.loop(1, 7)(functools.partial(step_z, level=level, done=True))

    @pl.loop(0, CHUNKS)
    def _(c):
        local_copy, remote_copy = out_copies(c)
        local_copy.wait()
        remote_copy.wait()


def local_fused(
    count, block_input, gate, q_fresh, kv_fresh, kv_cache, active_list, active_count, key_list, out_weight
):
    tok, width = block_input.shape
    own_side = lax.axis_index("blk")
    tiles = active_list.shape[2]
    flags = tile_flags(active_list[0, own_side], active_count[0, own_side])
    row_flags = jnp.repeat(flags, tok // tiles, total_repeat_length=tok)
    resident = jnp.where(row_flags[:, None, None], kv_fresh, kv_cache)
    rows = out_weight.shape[0]
    half = width // 2
    columns = q_fresh.shape[1]
    smem = pl.BlockSpec(memory_space=pltpu.SMEM)
    anywhere = pl.BlockSpec(memory_space=pl.ANY)
    dma = pltpu.SemaphoreType.DMA
    return pl.pallas_call(
        functools.partial(fused, count // LINE),
        out_shape=jax.ShapeDtypeStruct((tok, width), jnp.bfloat16),
        in_specs=[smem] * 3
        + [anywhere, pl.BlockSpec(memory_space=pltpu.VMEM)]
        + [anywhere] * 4,
        out_specs=anywhere,
        scratch_shapes=[
            pltpu.VMEM((CHUNKS, count * rows, half // CHUNKS), jnp.bfloat16),
            pltpu.VMEM((tok, columns), jnp.bfloat16),
            pltpu.VMEM((2 * tok, columns), jnp.bfloat16),
            pltpu.VMEM((2 * tok, columns), jnp.bfloat16),
            pltpu.VMEM((2 * tok, columns), jnp.bfloat16),
            pltpu.VMEM((2 * tok, half), jnp.bfloat16),
            pltpu.VMEM((CHUNKS, 2 * tok, half // CHUNKS), jnp.bfloat16),
            pltpu.VMEM((tok, 2 * tok), jnp.float32),
            dma((4,)),
            dma((CHUNKS,)),
            dma((4,)),
            dma((4,)),
            dma((CHUNKS, count, 4)),
            dma((CHUNKS, count)),
            dma((CHUNKS,)),
            dma((CHUNKS,)),
            dma((CHUNKS,)),
        ],
        compiler_params=pltpu.CompilerParams(
            collective_id=0, has_side_effects=True, vmem_limit_bytes=60 * 1024 * 1024
        ),
    )(
        active_list,
        active_count,
        key_list,
        block_input,
        gate[None, :],
        q_fresh,
        resident[:, 0],
        resident[:, 1],
        out_weight,
    )


def per_device(groups, count, cores, *args):
    rows, width = args[-1].shape
    fits = groups == 2 and cores == 2 and count % LINE == 0 and rows % 16 == 0
    fits = fits and width % (2 * CHUNKS * 128) == 0 and count * rows * width < 1 << 24
    return local_fused(count, *args) if fits else local(*args)


def solution(mesh):
    in_specs = (
        P(("groups", "fsdp", "blk"), None),
        P("groups"),
        P(("groups", "fsdp", "blk"), None),
        P(("groups", "fsdp", "blk"), None, None),
        P(("groups", "fsdp", "blk"), None, None),
        P(("groups", "fsdp"), None, None),
        P(("groups", "fsdp"), None),
        P(("groups", "fsdp"), None, None),
        P("fsdp", None),
    )
    sizes = [mesh.shape[axis] for axis in ("groups", "fsdp", "blk")]
    body = functools.partial(per_device, *sizes)
    out_specs = P(("groups", "fsdp", "blk"), None)
    return jax.shard_map(body, mesh=mesh, in_specs=in_specs, out_specs=out_specs, check_vma=False)
```

```python
import functools
import math

import jax
import jax.numpy as jnp
from jax import lax
from jax.experimental import pallas as pl
from jax.experimental.pallas import tpu as pltpu
from jax.sharding import PartitionSpec as P

HEADS = 20
HEAD_DIM = 128


MASKED = -1e30


def swapped(block, axis, apart):
    count = lax.axis_size(axis)
    route = []
    for low in range(count):
        high = low | 1 << apart
        if high != low and high < count:
            route += [(low, high), (high, low)]
    return lax.ppermute(block, axis, route)


def tile_flags(tile_list, tile_count):
    slot_ids = jnp.arange(tile_list.shape[0], dtype=jnp.int32)
    listed = (tile_list[:, None] == slot_ids[None, :]) & (slot_ids[:, None] < tile_count)
    return jnp.any(listed, axis=0)


def block_partial(query_tile, key_rows, value_rows, allowed):
    tile_rows = query_tile.shape[0]
    query3 = query_tile.reshape(tile_rows, HEADS, HEAD_DIM)
    key3 = key_rows.reshape(key_rows.shape[0], HEADS, HEAD_DIM)
    value3 = value_rows.reshape(value_rows.shape[0], HEADS, HEAD_DIM)
    scores = jnp.einsum(
        "qhd,khd->hqk", query3, key3, preferred_element_type=jnp.float32
    ) / math.sqrt(HEAD_DIM)
    scores = jnp.where(allowed[None, None, :], scores, MASKED)
    row_max = jnp.max(scores, axis=2)
    exp_terms = jnp.where(allowed[None, None, :], jnp.exp(scores - row_max[:, :, None]), 0.0)
    row_total = jnp.sum(exp_terms, axis=2)
    weights = exp_terms.astype(jnp.bfloat16)
    block_out = jnp.einsum("hqk,khd->hqd", weights, value3, preferred_element_type=jnp.float32)
    return (block_out, row_max, row_total)


def attend_block(
    queries, tile_list, tile_count, query_side, key_rows, value_rows, key_side, key_table
):
    tiles_dev = tile_list.shape[0]
    tile_rows = queries.shape[0] // tiles_dev
    slot_ids = jnp.arange(tiles_dev, dtype=jnp.int32)
    key_tiles = key_side * tiles_dev + slot_ids
    init_state = (
        jnp.zeros((tiles_dev, HEADS, tile_rows, HEAD_DIM), jnp.float32),
        jnp.full((tiles_dev, HEADS, tile_rows), MASKED, jnp.float32),
        jnp.zeros((tiles_dev, HEADS, tile_rows), jnp.float32),
    )

    def one_slot(slot_idx, carry_state):
        tile_pos = tile_list[slot_idx]
        query_tile = lax.dynamic_slice_in_dim(queries, tile_pos * tile_rows, tile_rows, 0)
        listed = key_table[query_side * tiles_dev + tile_pos]
        allowed_tiles = jnp.any(key_tiles[:, None] == listed[None, :], axis=1)
        allowed = jnp.repeat(allowed_tiles, tile_rows, total_repeat_length=tiles_dev * tile_rows)
        partial_value = block_partial(query_tile, key_rows, value_rows, allowed)
        return tuple(
            (whole.at[tile_pos].set(piece) for whole, piece in zip(carry_state, partial_value))
        )

    return lax.fori_loop(0, tile_count, one_slot, init_state)


def merge_states(earlier, later_state):
    out_one, max_one, total_one = earlier
    out_two, max_two, total_two = later_state
    joint_max = jnp.maximum(max_one, max_two)
    scale_one = jnp.exp(max_one - joint_max)
    scale_two = jnp.exp(max_two - joint_max)
    summed = out_one * scale_one[..., None] + out_two * scale_two[..., None]
    return (summed, total_one * scale_one + total_two * scale_two)


def local(
    block_input, gate, q_fresh, kv_fresh, kv_cache, active_list, active_count, key_list, out_weight
):
    own_side = lax.axis_index("blk")
    other_side = 1 - own_side
    tiles_dev = active_list.shape[2]
    tok_dev = block_input.shape[0]
    tile_rows = tok_dev // tiles_dev
    own_list = active_list[0, own_side]
    own_count = active_count[0, own_side]
    flags = tile_flags(own_list, own_count)
    row_flags = jnp.repeat(flags, tile_rows, total_repeat_length=tok_dev)
    resident = jnp.where(row_flags[:, None, None], kv_fresh, kv_cache)
    key_table = key_list[0]
    own_state = attend_block(
        q_fresh, own_list, own_count, own_side, resident[:, 0], resident[:, 1], own_side, key_table
    )
    other_kv = swapped(resident, "blk", 0)
    other_state = attend_block(
        q_fresh,
        own_list,
        own_count,
        own_side,
        other_kv[:, 0],
        other_kv[:, 1],
        other_side,
        key_table,
    )
    summed, denom = merge_states(own_state, other_state)
    denom = jnp.where(flags[:, None, None], denom, 1.0)
    attended = (
        (summed / denom[..., None])
        .transpose(0, 2, 1, 3)
        .reshape(tok_dev, HEADS * HEAD_DIM)
        .astype(jnp.bfloat16)
    )
    half_cols = out_weight.shape[1] // 2
    own_cols = lax.dynamic_slice_in_dim(out_weight, own_side * half_cols, half_cols, 1)
    half_weight = lax.all_gather(own_cols, "fsdp", axis=0, tiled=True)
    partner_rows = swapped(attended, "blk", 0)
    own_part = jnp.dot(attended, half_weight, preferred_element_type=jnp.float32)
    partner_part = jnp.dot(partner_rows, half_weight, preferred_element_type=jnp.float32)
    returned = swapped(partner_part, "blk", 0)
    projected = jnp.where(
        own_side == 0,
        jnp.concatenate([own_part, returned], axis=1),
        jnp.concatenate([returned, own_part], axis=1),
    )
    mixed = block_input.astype(jnp.float32) + gate[None, :] * projected
    return jnp.where(row_flags[:, None], mixed.astype(jnp.bfloat16), block_input)

MESH = pl.DeviceIdType.MESH
CHUNKS = 10
LINE = 2


def fused(
    depth,
    active_list,
    active_count,
    key_list,
    block_hbm,
    gate_ref,
    q_hbm,
    fresh_hbm,
    cache_hbm,
    w_hbm,
    out_hbm,
    weight,
    queries,
    fresh,
    cache,
    wide,
    keys,
    values,
    attended,
    mixed_in,
    mixed_out,
    mask,
    load_sem,
    w_sem,
    pair_send,
    pair_recv,
    send_sem,
    recv_sem,
    store_sem,
    out_send,
    out_recv,
):
    me = lax.axis_index("fsdp")
    z, x = me // LINE, me % LINE
    y = lax.axis_index("groups")
    b = lax.axis_index("blk")
    rows = w_hbm.shape[0]
    tok = q_hbm.shape[0]
    half = w_hbm.shape[1] // 2
    width = half // CHUNKS
    tiles = active_list.shape[2]
    tile_rows = tok // tiles
    heads = q_hbm.shape[1] // HEAD_DIM
    mine = pl.multiple_of(b * half, 128)
    theirs = pl.multiple_of((1 - b) * half, 128)

    barrier = pltpu.get_barrier_semaphore()
    targets = (
        (z < depth - 1, {"fsdp": me + LINE}),
        (z > 0, {"fsdp": me - LINE}),
        (None, {"fsdp": z * LINE + 1 - x}),
        (None, {"groups": 1 - y}),
    )
    core = {"blk": 1 - b}

    def when(cond, body):
        if cond is None:
            body()
        else:
            pl.when(cond)(body)

    def greet(device):
        pl.semaphore_signal(barrier, inc=1, device_id=device, device_id_type=MESH)

    for cond, device in targets + ((None, core),):
        when(cond, functools.partial(greet, device))

    def own_weight(c):
        return pltpu.make_async_copy(
            w_hbm.at[:, pl.ds(pl.multiple_of(mine + c * width, 128), width)],
            weight.at[c, pl.ds(pl.multiple_of(me * rows, 16), rows), :],
            w_sem.at[c],
        )

    def stream(i):
        return jnp.where(i == 0, y, jnp.where(i < 3, 1 + 2 * y + i, 3 + i))

    def passive(i):
        return jnp.where(i == 0, 1 - y, 3 - 2 * y + i)

    def every(i):
        return jnp.where(i < 7, stream(i), passive(i - 7))

    for i in range(CHUNKS):
        own_weight(every(jnp.int32(i))).start()

    loads = [
        pltpu.make_async_copy(q_hbm, queries, load_sem.at[0]),
        pltpu.make_async_copy(fresh_hbm, fresh.at[pl.ds(0, tok)], load_sem.at[1]),
        pltpu.make_async_copy(cache_hbm, cache.at[pl.ds(0, tok)], load_sem.at[2]),
        pltpu.make_async_copy(
            block_hbm.at[:, pl.ds(mine, half)], mixed_in.at[pl.ds(0, tok)], load_sem.at[3]
        ),
    ]
    for load in loads:
        load.start()

    pl.semaphore_wait(barrier, 3 + (z > 0).astype(jnp.int32) + (z < depth - 1).astype(jnp.int32))

    def to_core(src, dst, index):
        return pltpu.make_async_remote_copy(
            src_ref=src,
            dst_ref=dst,
            send_sem=pair_send.at[index],
            recv_sem=pair_recv.at[index],
            device_id=core,
            device_id_type=MESH,
        )

    swaps = [
        to_core(fresh_hbm, fresh.at[pl.ds(tok, tok)], 0),
        to_core(cache_hbm, cache.at[pl.ds(tok, tok)], 1),
        to_core(block_hbm.at[:, pl.ds(theirs, half)], mixed_in.at[pl.ds(tok, tok)], 2),
    ]
    give = to_core(attended.at[pl.ds(0, tok)], attended.at[pl.ds(tok, tok)], 3)
    for swap in swaps:
        swap.start()

    def shard_copy(c, s, way):
        block = weight.at[c, pl.ds(pl.multiple_of(s * rows, 16), rows), :]
        return pltpu.make_async_remote_copy(
            src_ref=block,
            dst_ref=block,
            send_sem=send_sem.at[c, s, way],
            recv_sem=recv_sem.at[c, s],
            device_id=targets[way][1],
            device_id_type=MESH,
        )

    def visit(c, first, over_y, dz, dx, done):
        s = (z + dz) * LINE + (x if dx == 0 else 1 - x)
        ways = []
        if first == "z":
            if dx == 0:
                ways += [0] if dz <= 0 else []
                ways += [1] if dz >= 0 else []
                ways += [2]
        else:
            ways += [2] if (dz, dx) == (0, 0) else []
            ways += [0] if dz <= 0 else []
            ways += [1] if dz >= 0 else []

        def body():
            if (dz, dx) == (0, 0):
                if not done:
                    own_weight(c).wait()
            elif not done:
                shard_copy(c, s, 2).wait_recv()

            def act(way):
                copy = shard_copy(c, s, way)
                if done:
                    copy.wait_send()
                else:
                    copy.start()

            for way in ways:
                when(targets[way][0], functools.partial(act, way))
            if (dz, dx) != (0, 0) and over_y is not False:
                when(None if over_y is True else over_y, functools.partial(act, 3))

        if dz < 0:
            pl.when(z + dz >= 0)(body)
        elif dz > 0:
            pl.when(z + dz < depth)(body)
        else:
            body()

    def offsets(level):
        found = []
        for dx in range(LINE):
            far = level - dx
            if 0 <= far < depth:
                found += [(0, dx)] if far == 0 else [(-far, dx), (far, dx)]
        return found

    levels = depth + LINE - 1

    def step_x(level, done=False):
        for dz, dx in offsets(level):
            visit(y, "x", True, dz, dx, done)

    def step_z(i, level, done=False):
        for dz, dx in offsets(level):
            visit(stream(i), "z", i < 3, dz, dx, done)

    step_x(0)
    pl.loop(1, 7)(lambda i: step_z(i, 0))

    def is_active(side, a):
        found = jnp.int32(0)
        for slot in range(tiles):
            hit = (active_list[0, side, slot] == a) & (slot < active_count[0, side])
            found = jnp.where(hit, jnp.int32(1), found)
        return found

    flags = [is_active(side, a) for side in (b, 1 - b) for a in range(tiles)]

    def settle(side, h):
        cols = pl.ds(pl.multiple_of(h * HEAD_DIM, 128), HEAD_DIM)
        for a in range(tiles):
            place = side * tiles + a
            span = pl.ds(place * tile_rows, tile_rows)
            pair = jnp.where(flags[place] > 0, fresh[span, :, cols], cache[span, :, cols])
            pair = pair.reshape(2 * tile_rows, HEAD_DIM)
            wide[pl.ds(2 * a * tile_rows, 2 * tile_rows), :] = pair.astype(jnp.float32)
        whole = pl.ds(side * tok, tok)
        keys[whole, cols] = wide[pl.ds(0, tok, 2), :].astype(jnp.bfloat16)
        values[whole, cols] = wide[pl.ds(1, tok, 2), :].astype(jnp.bfloat16)

    for load in loads[:3]:
        load.wait()
    pl.loop(0, heads)(functools.partial(settle, 0))
    for swap in swaps[:2]:
        swap.wait_recv()
    pl.loop(0, heads)(functools.partial(settle, 1))

    for a in range(tiles):
        for t in range(2 * tiles):
            side = b if t < tiles else 1 - b
            tile_id = side * tiles + t % tiles
            listed = jnp.int32(0)
            for slot in range(key_list.shape[0]):
                hit = key_list[slot, 0, b * tiles + a] == tile_id
                listed = jnp.where(hit, jnp.int32(1), listed)
            mask[pl.ds(a * tile_rows, tile_rows), pl.ds(t * tile_rows, tile_rows)] = jnp.full(
                (tile_rows, tile_rows), listed.astype(jnp.float32), jnp.float32
            )

    def attend(h):
        cols = pl.ds(pl.multiple_of(h * HEAD_DIM, 128), HEAD_DIM)
        query = queries[:, cols]
        parts = []
        for side in range(2):
            span = pl.ds(side * tok, tok)
            scores = lax.dot_general(
                query,
                keys[span, cols],
                (((1,), (1,)), ((), ())),
                preferred_element_type=jnp.float32,
            ) * (1.0 / math.sqrt(HEAD_DIM))
            allowed = mask[:, span] > 0.5
            scores = jnp.where(allowed, scores, MASKED)
            top = jnp.max(scores, axis=1, keepdims=True)
            terms = jnp.where(allowed, jnp.exp(scores - top), 0.0)
            total = jnp.sum(terms, axis=1, keepdims=True)
            part = jnp.dot(
                terms.astype(jnp.bfloat16), values[span, cols], preferred_element_type=jnp.float32
            )
            parts.append((part, top, total))
        (out0, max0, sum0), (out1, max1, sum1) = parts
        joint = jnp.maximum(max0, max1)
        scale0 = jnp.exp(max0 - joint)
        scale1 = jnp.exp(max1 - joint)
        denom = sum0 * scale0 + sum1 * scale1
        result = (out0 * scale0 + out1 * scale1) / denom
        attended[pl.ds(0, tok), cols] = result.astype(jnp.bfloat16)

    def attend_range(low, high):
        pl.loop(low, high)(attend)

    each = heads // 7
    first = heads - 6 * each
    step_x(1)
    attend_range(0, first)

    @pl.loop(1, 7)
    def _(i):
        step_z(i, 1)
        attend_range(first + (i - 1) * each, first + i * each)

    give.start()
    for level in range(2, levels - 1):
        step_x(level)
        pl.loop(1, 7)(functools.partial(step_z, level=level))

    loads[3].wait()
    swaps[2].wait_recv()
    give.wait_recv()

    def out_copies(c):
        cols = pl.ds(pl.multiple_of(mine + c * width, 128), width)
        return (
            pltpu.make_async_copy(
                mixed_out.at[c, pl.ds(0, tok), :], out_hbm.at[:, cols], store_sem.at[c]
            ),
            pltpu.make_async_remote_copy(
                src_ref=mixed_out.at[c, pl.ds(tok, tok), :],
                dst_ref=out_hbm.at[:, cols],
                send_sem=out_send.at[c],
                recv_sem=out_recv.at[c],
                device_id=core,
                device_id_type=MESH,
            ),
        )

    def project(j):
        i = jnp.where(j < 3, j, jnp.where(j < 6, j + 4, j - 3))
        c = every(i)

        @pl.when(j == 0)
        def _():
            step_x(levels - 1)

        @pl.when((j == 1) | (j == 2) | (j >= 6))
        def _():
            step_z(i, levels - 1)

        @pl.when((j >= 3) & (j < 6))
        def _():
            own_weight(c).wait()
            for s in range(depth * LINE):
                pl.when(me != s)(lambda s=s: shard_copy(c, s, 3).wait_recv())

        projected = jnp.dot(attended[...], weight[c], preferred_element_type=jnp.float32)
        gate = gate_ref[:, pl.ds(pl.multiple_of(mine + c * width, 128), width)]
        cols = pl.ds(pl.multiple_of(c * width, 128), width)
        for place, flag in enumerate(flags):
            span = pl.ds(place * tile_rows, tile_rows)
            before = mixed_in[span, cols].astype(jnp.float32)
            part = projected[place * tile_rows : (place + 1) * tile_rows]
            mixed = jnp.where(flag > 0, before + gate * part, before)
            mixed_out[c, span, :] = mixed.astype(jnp.bfloat16)
        for copy in out_copies(c):
            copy.start()

    pl.loop(0, CHUNKS)(project)

    for swap in swaps + [give]:
        swap.wait_send()
    for level in range(levels):
        step_x(level, done=True)
        pl.loop(1, 7)(functools.partial(step_z, level=level, done=True))

    @pl.loop(0, CHUNKS)
    def _(c):
        local_copy, remote_copy = out_copies(c)
        local_copy.wait()
        remote_copy.wait()


def local_fused(
    count, block_input, gate, q_fresh, kv_fresh, kv_cache, active_list, active_count, key_list, out_weight
):
    tok, width = block_input.shape
    rows = out_weight.shape[0]
    half = width // 2
    columns = q_fresh.shape[1]
    smem = pl.BlockSpec(memory_space=pltpu.SMEM)
    anywhere = pl.BlockSpec(memory_space=pltpu.HBM)
    dma = pltpu.SemaphoreType.DMA
    return pl.pallas_call(
        functools.partial(fused, count // LINE),
        out_shape=jax.ShapeDtypeStruct((tok, width), jnp.bfloat16),
        in_specs=[smem] * 3
        + [anywhere, pl.BlockSpec(memory_space=pltpu.VMEM)]
        + [anywhere] * 4,
        out_specs=pl.BlockSpec(memory_space=pl.ANY),
        scratch_shapes=[
            pltpu.VMEM((CHUNKS, count * rows, half // CHUNKS), jnp.bfloat16),
            pltpu.VMEM((tok, columns), jnp.bfloat16),
            pltpu.VMEM((2 * tok, 2, columns), jnp.bfloat16),
            pltpu.VMEM((2 * tok, 2, columns), jnp.bfloat16),
            pltpu.VMEM((2 * tok, HEAD_DIM), jnp.float32),
            pltpu.VMEM((2 * tok, columns), jnp.bfloat16),
            pltpu.VMEM((2 * tok, columns), jnp.bfloat16),
            pltpu.VMEM((2 * tok, columns), jnp.bfloat16),
            pltpu.VMEM((2 * tok, half), jnp.bfloat16),
            pltpu.VMEM((CHUNKS, 2 * tok, half // CHUNKS), jnp.bfloat16),
            pltpu.VMEM((tok, 2 * tok), jnp.float32),
            dma((4,)),
            dma((CHUNKS,)),
            dma((4,)),
            dma((4,)),
            dma((CHUNKS, count, 4)),
            dma((CHUNKS, count)),
            dma((CHUNKS,)),
            dma((CHUNKS,)),
            dma((CHUNKS,)),
        ],
        compiler_params=pltpu.CompilerParams(
            collective_id=0, has_side_effects=True, vmem_limit_bytes=60000000
        ),
    )(
        active_list,
        active_count,
        key_list.transpose(2, 0, 1),
        block_input,
        gate[None, :],
        q_fresh,
        kv_fresh,
        kv_cache,
        out_weight,
    )


def per_device(groups, count, cores, *args):
    rows, width = args[-1].shape
    fits = groups == 2 and cores == 2 and count % LINE == 0 and rows % 16 == 0
    fits = fits and width % (2 * CHUNKS * 128) == 0 and count * rows * width < 1 << 24
    return local_fused(count, *args) if fits else local(*args)


def solution(mesh):
    in_specs = (
        P(("groups", "fsdp", "blk"), None),
        P("groups"),
        P(("groups", "fsdp", "blk"), None),
        P(("groups", "fsdp", "blk"), None, None),
        P(("groups", "fsdp", "blk"), None, None),
        P(("groups", "fsdp"), None, None),
        P(("groups", "fsdp"), None),
        P(("groups", "fsdp"), None, None),
        P("fsdp", None),
    )
    sizes = [mesh.shape[axis] for axis in ("groups", "fsdp", "blk")]
    body = functools.partial(per_device, *sizes)
    out_specs = P(("groups", "fsdp", "blk"), None)
    return jax.shard_map(body, mesh=mesh, in_specs=in_specs, out_specs=out_specs, check_vma=False)
```

```python
import functools
import math

import jax
import jax.numpy as jnp
from jax import lax
from jax.experimental import pallas as pl
from jax.experimental.pallas import tpu as pltpu
from jax.sharding import PartitionSpec as P

HEADS = 20
HEAD_DIM = 128


MASKED = -1e30


def swapped(block, axis, apart):
    count = lax.axis_size(axis)
    route = []
    for low in range(count):
        high = low | 1 << apart
        if high != low and high < count:
            route += [(low, high), (high, low)]
    return lax.ppermute(block, axis, route)


def tile_flags(tile_list, tile_count):
    slot_ids = jnp.arange(tile_list.shape[0], dtype=jnp.int32)
    listed = (tile_list[:, None] == slot_ids[None, :]) & (slot_ids[:, None] < tile_count)
    return jnp.any(listed, axis=0)


def block_partial(query_tile, key_rows, value_rows, allowed):
    tile_rows = query_tile.shape[0]
    query3 = query_tile.reshape(tile_rows, HEADS, HEAD_DIM)
    key3 = key_rows.reshape(key_rows.shape[0], HEADS, HEAD_DIM)
    value3 = value_rows.reshape(value_rows.shape[0], HEADS, HEAD_DIM)
    scores = jnp.einsum(
        "qhd,khd->hqk", query3, key3, preferred_element_type=jnp.float32
    ) / math.sqrt(HEAD_DIM)
    scores = jnp.where(allowed[None, None, :], scores, MASKED)
    row_max = jnp.max(scores, axis=2)
    exp_terms = jnp.where(allowed[None, None, :], jnp.exp(scores - row_max[:, :, None]), 0.0)
    row_total = jnp.sum(exp_terms, axis=2)
    weights = exp_terms.astype(jnp.bfloat16)
    block_out = jnp.einsum("hqk,khd->hqd", weights, value3, preferred_element_type=jnp.float32)
    return (block_out, row_max, row_total)


def attend_block(
    queries, tile_list, tile_count, query_side, key_rows, value_rows, key_side, key_table
):
    tiles_dev = tile_list.shape[0]
    tile_rows = queries.shape[0] // tiles_dev
    slot_ids = jnp.arange(tiles_dev, dtype=jnp.int32)
    key_tiles = key_side * tiles_dev + slot_ids
    init_state = (
        jnp.zeros((tiles_dev, HEADS, tile_rows, HEAD_DIM), jnp.float32),
        jnp.full((tiles_dev, HEADS, tile_rows), MASKED, jnp.float32),
        jnp.zeros((tiles_dev, HEADS, tile_rows), jnp.float32),
    )

    def one_slot(slot_idx, carry_state):
        tile_pos = tile_list[slot_idx]
        query_tile = lax.dynamic_slice_in_dim(queries, tile_pos * tile_rows, tile_rows, 0)
        listed = key_table[query_side * tiles_dev + tile_pos]
        allowed_tiles = jnp.any(key_tiles[:, None] == listed[None, :], axis=1)
        allowed = jnp.repeat(allowed_tiles, tile_rows, total_repeat_length=tiles_dev * tile_rows)
        partial_value = block_partial(query_tile, key_rows, value_rows, allowed)
        return tuple(
            (whole.at[tile_pos].set(piece) for whole, piece in zip(carry_state, partial_value))
        )

    return lax.fori_loop(0, tile_count, one_slot, init_state)


def merge_states(earlier, later_state):
    out_one, max_one, total_one = earlier
    out_two, max_two, total_two = later_state
    joint_max = jnp.maximum(max_one, max_two)
    scale_one = jnp.exp(max_one - joint_max)
    scale_two = jnp.exp(max_two - joint_max)
    summed = out_one * scale_one[..., None] + out_two * scale_two[..., None]
    return (summed, total_one * scale_one + total_two * scale_two)


def local(
    block_input, gate, q_fresh, kv_fresh, kv_cache, active_list, active_count, key_list, out_weight
):
    own_side = lax.axis_index("blk")
    other_side = 1 - own_side
    tiles_dev = active_list.shape[2]
    tok_dev = block_input.shape[0]
    tile_rows = tok_dev // tiles_dev
    own_list = active_list[0, own_side]
    own_count = active_count[0, own_side]
    flags = tile_flags(own_list, own_count)
    row_flags = jnp.repeat(flags, tile_rows, total_repeat_length=tok_dev)
    resident = jnp.where(row_flags[:, None, None], kv_fresh, kv_cache)
    key_table = key_list[0]
    own_state = attend_block(
        q_fresh, own_list, own_count, own_side, resident[:, 0], resident[:, 1], own_side, key_table
    )
    other_kv = swapped(resident, "blk", 0)
    other_state = attend_block(
        q_fresh,
        own_list,
        own_count,
        own_side,
        other_kv[:, 0],
        other_kv[:, 1],
        other_side,
        key_table,
    )
    summed, denom = merge_states(own_state, other_state)
    denom = jnp.where(flags[:, None, None], denom, 1.0)
    attended = (
        (summed / denom[..., None])
        .transpose(0, 2, 1, 3)
        .reshape(tok_dev, HEADS * HEAD_DIM)
        .astype(jnp.bfloat16)
    )
    half_cols = out_weight.shape[1] // 2
    own_cols = lax.dynamic_slice_in_dim(out_weight, own_side * half_cols, half_cols, 1)
    half_weight = lax.all_gather(own_cols, "fsdp", axis=0, tiled=True)
    partner_rows = swapped(attended, "blk", 0)
    own_part = jnp.dot(attended, half_weight, preferred_element_type=jnp.float32)
    partner_part = jnp.dot(partner_rows, half_weight, preferred_element_type=jnp.float32)
    returned = swapped(partner_part, "blk", 0)
    projected = jnp.where(
        own_side == 0,
        jnp.concatenate([own_part, returned], axis=1),
        jnp.concatenate([returned, own_part], axis=1),
    )
    mixed = block_input.astype(jnp.float32) + gate[None, :] * projected
    return jnp.where(row_flags[:, None], mixed.astype(jnp.bfloat16), block_input)

MESH = pl.DeviceIdType.MESH
CHUNKS = 20
TURNED = 2
SHARED = 4
HELD = TURNED + SHARED
STREAMS = CHUNKS - HELD
LINE = 2


def fused(
    depth,
    active_list,
    active_count,
    key_list,
    block_hbm,
    gate_ref,
    q_hbm,
    fresh_hbm,
    cache_hbm,
    w_hbm,
    out_hbm,
    weight,
    queries,
    fresh,
    cache,
    wide,
    keys,
    values,
    attended,
    mixed_in,
    mixed_out,
    mask,
    load_sem,
    w_sem,
    pair_send,
    pair_recv,
    send_sem,
    recv_sem,
    store_sem,
    out_send,
    out_recv,
):
    me = lax.axis_index("fsdp")
    z, x = me // LINE, me % LINE
    y = lax.axis_index("groups")
    b = lax.axis_index("blk")
    rows = w_hbm.shape[0]
    tok = q_hbm.shape[0]
    half = w_hbm.shape[1] // 2
    width = half // CHUNKS
    tiles = active_list.shape[2]
    tile_rows = tok // tiles
    heads = q_hbm.shape[1] // HEAD_DIM
    mine = pl.multiple_of(b * half, 128)
    theirs = pl.multiple_of((1 - b) * half, 128)

    barrier = pltpu.get_barrier_semaphore()
    targets = (
        (z < depth - 1, {"fsdp": me + LINE}),
        (z > 0, {"fsdp": me - LINE}),
        (None, {"fsdp": z * LINE + 1 - x}),
        (None, {"groups": 1 - y}),
    )
    core = {"blk": 1 - b}

    def when(cond, body):
        if cond is None:
            body()
        else:
            pl.when(cond)(body)

    def greet(device):
        pl.semaphore_signal(barrier, inc=1, device_id=device, device_id_type=MESH)

    for cond, device in targets + ((None, core),):
        when(cond, functools.partial(greet, device))

    def own_weight(c):
        return pltpu.make_async_copy(
            w_hbm.at[:, pl.ds(pl.multiple_of(mine + c * width, 128), width)],
            weight.at[c, pl.ds(pl.multiple_of(me * rows, 16), rows), :],
            w_sem.at[c],
        )

    def held(i, owner):
        return jnp.where(i < TURNED, owner * TURNED + i, TURNED + owner * SHARED + i)

    def stream(i):
        return jnp.where(i < HELD, held(i, y), HELD + i)

    def every(i):
        return jnp.where(i < STREAMS, stream(i), held(i - STREAMS, 1 - y))

    for i in range(CHUNKS):
        own_weight(every(jnp.int32(i))).start()

    loads = [
        pltpu.make_async_copy(q_hbm, queries, load_sem.at[0]),
        pltpu.make_async_copy(fresh_hbm, fresh.at[pl.ds(0, tok)], load_sem.at[1]),
        pltpu.make_async_copy(cache_hbm, cache.at[pl.ds(0, tok)], load_sem.at[2]),
        pltpu.make_async_copy(
            block_hbm.at[:, pl.ds(mine, half)], mixed_in.at[pl.ds(0, tok)], load_sem.at[3]
        ),
    ]
    for load in loads:
        load.start()

    pl.semaphore_wait(barrier, 3 + (z > 0).astype(jnp.int32) + (z < depth - 1).astype(jnp.int32))

    def to_core(src, dst, index):
        return pltpu.make_async_remote_copy(
            src_ref=src,
            dst_ref=dst,
            send_sem=pair_send.at[index],
            recv_sem=pair_recv.at[index],
            device_id=core,
            device_id_type=MESH,
        )

    swaps = [
        to_core(fresh_hbm, fresh.at[pl.ds(tok, tok)], 0),
        to_core(cache_hbm, cache.at[pl.ds(tok, tok)], 1),
        to_core(block_hbm.at[:, pl.ds(theirs, half)], mixed_in.at[pl.ds(tok, tok)], 2),
    ]
    give = to_core(attended.at[pl.ds(0, tok)], attended.at[pl.ds(tok, tok)], 3)
    for swap in swaps:
        swap.start()

    def shard_copy(c, s, way):
        block = weight.at[c, pl.ds(pl.multiple_of(s * rows, 16), rows), :]
        return pltpu.make_async_remote_copy(
            src_ref=block,
            dst_ref=block,
            send_sem=send_sem.at[c, s, way],
            recv_sem=recv_sem.at[c, s],
            device_id=targets[way][1],
            device_id_type=MESH,
        )

    def visit(c, first, over_y, dz, dx, done):
        s = (z + dz) * LINE + (x if dx == 0 else 1 - x)
        ways = []
        if first == "z":
            if dx == 0:
                ways += [0] if dz <= 0 else []
                ways += [1] if dz >= 0 else []
                ways += [2]
        else:
            ways += [2] if (dz, dx) == (0, 0) else []
            ways += [0] if dz <= 0 else []
            ways += [1] if dz >= 0 else []

        def body():
            if (dz, dx) == (0, 0):
                if not done:
                    own_weight(c).wait()
            elif not done:
                shard_copy(c, s, 2).wait_recv()

            def act(way):
                copy = shard_copy(c, s, way)
                if done:
                    copy.wait_send()
                else:
                    copy.start()

            for way in ways:
                when(targets[way][0], functools.partial(act, way))
            if (dz, dx) != (0, 0) and over_y is not False:
                when(None if over_y is True else over_y, functools.partial(act, 3))

        if dz < 0:
            pl.when(z + dz >= 0)(body)
        elif dz > 0:
            pl.when(z + dz < depth)(body)
        else:
            body()

    def offsets(level):
        found = []
        for dx in range(LINE):
            far = level - dx
            if 0 <= far < depth:
                found += [(0, dx)] if far == 0 else [(-far, dx), (far, dx)]
        return found

    levels = depth + LINE - 1

    def step_x(i, level, done=False):
        for dz, dx in offsets(level):
            visit(stream(i), "x", True, dz, dx, done)

    def step_z(i, level, done=False):
        for dz, dx in offsets(level):
            visit(stream(i), "z", i < HELD, dz, dx, done)

    def all_steps(level, done=False):
        pl.loop(0, TURNED)(functools.partial(step_x, level=level, done=done))
        pl.loop(TURNED, STREAMS)(functools.partial(step_z, level=level, done=done))

    all_steps(0)

    def is_active(side, a):
        found = jnp.int32(0)
        for slot in range(tiles):
            hit = (active_list[0, side, slot] == a) & (slot < active_count[0, side])
            found = jnp.where(hit, jnp.int32(1), found)
        return found

    flags = [is_active(side, a) for side in (b, 1 - b) for a in range(tiles)]

    def settle(side, h):
        cols = pl.ds(pl.multiple_of(h * HEAD_DIM, 128), HEAD_DIM)
        for a in range(tiles):
            place = side * tiles + a
            span = pl.ds(place * tile_rows, tile_rows)
            pair = jnp.where(flags[place] > 0, fresh[span, :, cols], cache[span, :, cols])
            pair = pair.reshape(2 * tile_rows, HEAD_DIM)
            wide[pl.ds(2 * a * tile_rows, 2 * tile_rows), :] = pair.astype(jnp.float32)
        whole = pl.ds(side * tok, tok)
        keys[whole, cols] = wide[pl.ds(0, tok, 2), :].astype(jnp.bfloat16)
        values[whole, cols] = wide[pl.ds(1, tok, 2), :].astype(jnp.bfloat16)

    for load in loads[:3]:
        load.wait()
    pl.loop(0, heads)(functools.partial(settle, 0))
    for swap in swaps[:2]:
        swap.wait_recv()
    pl.loop(0, heads)(functools.partial(settle, 1))

    for a in range(tiles):
        for t in range(2 * tiles):
            side = b if t < tiles else 1 - b
            tile_id = side * tiles + t % tiles
            listed = jnp.int32(0)
            for slot in range(key_list.shape[0]):
                hit = key_list[slot, 0, b * tiles + a] == tile_id
                listed = jnp.where(hit, jnp.int32(1), listed)
            mask[pl.ds(a * tile_rows, tile_rows), pl.ds(t * tile_rows, tile_rows)] = jnp.full(
                (tile_rows, tile_rows), listed.astype(jnp.float32), jnp.float32
            )

    def attend(h):
        cols = pl.ds(pl.multiple_of(h * HEAD_DIM, 128), HEAD_DIM)
        query = queries[:, cols]
        parts = []
        for side in range(2):
            span = pl.ds(side * tok, tok)
            scores = lax.dot_general(
                query,
                keys[span, cols],
                (((1,), (1,)), ((), ())),
                preferred_element_type=jnp.float32,
            ) * (1.0 / math.sqrt(HEAD_DIM))
            allowed = mask[:, span] > 0.5
            scores = jnp.where(allowed, scores, MASKED)
            top = jnp.max(scores, axis=1, keepdims=True)
            terms = jnp.where(allowed, jnp.exp(scores - top), 0.0)
            total = jnp.sum(terms, axis=1, keepdims=True)
            part = jnp.dot(
                terms.astype(jnp.bfloat16), values[span, cols], preferred_element_type=jnp.float32
            )
            parts.append((part, top, total))
        (out0, max0, sum0), (out1, max1, sum1) = parts
        joint = jnp.maximum(max0, max1)
        scale0 = jnp.exp(max0 - joint)
        scale1 = jnp.exp(max1 - joint)
        denom = sum0 * scale0 + sum1 * scale1
        result = (out0 * scale0 + out1 * scale1) / denom
        attended[pl.ds(0, tok), cols] = result.astype(jnp.bfloat16)

    def attend_range(low, high):
        pl.loop(low, high)(attend)

    each = -(-heads // (STREAMS - TURNED))
    pl.loop(0, TURNED)(functools.partial(step_x, level=1))

    @pl.loop(TURNED, STREAMS)
    def _(i):
        step_z(i, 1)
        low = (i - TURNED) * each
        attend_range(jnp.minimum(low, heads), jnp.minimum(low + each, heads))

    give.start()
    for level in range(2, levels - 1):
        all_steps(level)

    loads[3].wait()
    swaps[2].wait_recv()
    give.wait_recv()

    def out_copies(c):
        cols = pl.ds(pl.multiple_of(mine + c * width, 128), width)
        return (
            pltpu.make_async_copy(
                mixed_out.at[c, pl.ds(0, tok), :], out_hbm.at[:, cols], store_sem.at[c]
            ),
            pltpu.make_async_remote_copy(
                src_ref=mixed_out.at[c, pl.ds(tok, tok), :],
                dst_ref=out_hbm.at[:, cols],
                send_sem=out_send.at[c],
                recv_sem=out_recv.at[c],
                device_id=core,
                device_id_type=MESH,
            ),
        )

    def project(j):
        t = j - HELD
        i = jnp.where(t % 2 == 0, HELD + t // 2, STREAMS + t // 2)
        i = jnp.where(t < 2 * HELD, i, t)
        i = jnp.where(t < 0, j, i)
        c = every(i)

        @pl.when(i < TURNED)
        def _():
            step_x(i, levels - 1)

        @pl.when((i >= TURNED) & (i < STREAMS))
        def _():
            step_z(i, levels - 1)

        @pl.when(i >= STREAMS)
        def _():
            own_weight(c).wait()
            for s in range(depth * LINE):
                pl.when(me != s)(lambda s=s: shard_copy(c, s, 3).wait_recv())

        projected = jnp.dot(attended[...], weight[c], preferred_element_type=jnp.float32)
        gate = gate_ref[:, pl.ds(pl.multiple_of(mine + c * width, 128), width)]
        cols = pl.ds(pl.multiple_of(c * width, 128), width)
        for place, flag in enumerate(flags):
            span = pl.ds(place * tile_rows, tile_rows)
            before = mixed_in[span, cols].astype(jnp.float32)
            part = projected[place * tile_rows : (place + 1) * tile_rows]
            mixed = jnp.where(flag > 0, before + gate * part, before)
            mixed_out[c, span, :] = mixed.astype(jnp.bfloat16)
        for copy in out_copies(c):
            copy.start()

    pl.loop(0, CHUNKS)(project)

    for swap in swaps + [give]:
        swap.wait_send()
    for level in range(levels):
        all_steps(level, done=True)

    @pl.loop(0, CHUNKS)
    def _(c):
        local_copy, remote_copy = out_copies(c)
        local_copy.wait()
        remote_copy.wait()


def local_fused(
    count, block_input, gate, q_fresh, kv_fresh, kv_cache, active_list, active_count, key_list, out_weight
):
    tok, width = block_input.shape
    rows = out_weight.shape[0]
    half = width // 2
    columns = q_fresh.shape[1]
    smem = pl.BlockSpec(memory_space=pltpu.SMEM)
    anywhere = pl.BlockSpec(memory_space=pltpu.HBM)
    dma = pltpu.SemaphoreType.DMA
    return pl.pallas_call(
        functools.partial(fused, count // LINE),
        out_shape=jax.ShapeDtypeStruct((tok, width), jnp.bfloat16),
        in_specs=[smem] * 3
        + [anywhere, pl.BlockSpec(memory_space=pltpu.VMEM)]
        + [anywhere] * 4,
        out_specs=pl.BlockSpec(memory_space=pl.ANY),
        scratch_shapes=[
            pltpu.VMEM((CHUNKS, count * rows, half // CHUNKS), jnp.bfloat16),
            pltpu.VMEM((tok, columns), jnp.bfloat16),
            pltpu.VMEM((2 * tok, 2, columns), jnp.bfloat16),
            pltpu.VMEM((2 * tok, 2, columns), jnp.bfloat16),
            pltpu.VMEM((2 * tok, HEAD_DIM), jnp.float32),
            pltpu.VMEM((2 * tok, columns), jnp.bfloat16),
            pltpu.VMEM((2 * tok, columns), jnp.bfloat16),
            pltpu.VMEM((2 * tok, columns), jnp.bfloat16),
            pltpu.VMEM((2 * tok, half), jnp.bfloat16),
            pltpu.VMEM((CHUNKS, 2 * tok, half // CHUNKS), jnp.bfloat16),
            pltpu.VMEM((tok, 2 * tok), jnp.float32),
            dma((4,)),
            dma((CHUNKS,)),
            dma((4,)),
            dma((4,)),
            dma((CHUNKS, count, 4)),
            dma((CHUNKS, count)),
            dma((CHUNKS,)),
            dma((CHUNKS,)),
            dma((CHUNKS,)),
        ],
        compiler_params=pltpu.CompilerParams(
            collective_id=0, has_side_effects=True, vmem_limit_bytes=60000000
        ),
    )(
        active_list,
        active_count,
        key_list.transpose(2, 0, 1),
        block_input,
        gate[None, :],
        q_fresh,
        kv_fresh,
        kv_cache,
        out_weight,
    )


def per_device(groups, count, cores, *args):
    rows, width = args[-1].shape
    fits = groups == 2 and cores == 2 and count % LINE == 0 and rows % 16 == 0
    fits = fits and width % (2 * CHUNKS * 128) == 0 and count * rows * width < 1 << 24
    return local_fused(count, *args) if fits else local(*args)


def solution(mesh):
    in_specs = (
        P(("groups", "fsdp", "blk"), None),
        P("groups"),
        P(("groups", "fsdp", "blk"), None),
        P(("groups", "fsdp", "blk"), None, None),
        P(("groups", "fsdp", "blk"), None, None),
        P(("groups", "fsdp"), None, None),
        P(("groups", "fsdp"), None),
        P(("groups", "fsdp"), None, None),
        P("fsdp", None),
    )
    sizes = [mesh.shape[axis] for axis in ("groups", "fsdp", "blk")]
    body = functools.partial(per_device, *sizes)
    out_specs = P(("groups", "fsdp", "blk"), None)
    return jax.shard_map(body, mesh=mesh, in_specs=in_specs, out_specs=out_specs, check_vma=False)
```
